256 devices in a mesh: row: 32 (over x, z), period: 8 (over y, core).
Axes of the slice: x: 4, y: 4, z: 8, core: 2. Of those that a mesh axis runs over, the one named last changes fastest.
Arguments:
- codes: int32 [8192, 64], P('row'), may hold values from 0 to 255
- node: int32 [8192], P('row'), may hold values from 0 to 15
- chosen: int32 [16, 32], replicated, may hold values from 0 to 63, all different within a row
- arm: int32 [8192], P('row'), may hold values 0 or 1
- honest: int32 [8192], P('row'), may hold values 0 or 1
- outcome: bfloat16 [8192, 128], P('row', 'period'), may hold values from -8 to 8
Outputs:
- gains: float32 [32, 16, 256], P('row', None, 'period')
- best_gain: float32 [16], replicated
- effect: float32 [16, 128], P(None, 'period')
The draws below stay inside these ranges and needn't reach their ends.
Inputs may be any that keep to these rules, and one draw needn't show every extreme that they name: Each row of chosen holds 32 different covariate ids.
All inputs are finite; a program needn't handle non-finite values. No bound on the sum of `arm` or of `honest` on one device may be relied on, other than what follows from the above.
Results may differ from the reference program's by a relative error of at most 0.001.
Values may be sent and summed in bfloat16 or wider, within the bound.
A program may use at most 64 MiB of HBM per device.

```python
import jax
import jax.numpy as jnp
from jax import lax

NODES = 16
SLOTS = 32
COVARS = 64
BINS = 256
WEEKS = 128
ROWS = 8192


def draw_outcome(key, part):
    key_base = jax.random.fold_in(key, 0)
    base = jax.random.normal(key_base, (ROWS, WEEKS), jnp.float32)
    position = jnp.arange(ROWS, dtype=jnp.float32) / ROWS
    row_scale = 0.5 * jnp.exp(jnp.log(3.0) * position)
    values = row_scale[:, None] * jnp.clip(base, -4.0, 4.0)
    return jnp.clip(values, -8.0, 8.0).astype(jnp.bfloat16)


def with_ends(array, key, low, largest):
    longest = array.shape.index(max(array.shape))
    spots = []
    for shift in (0, 1):
        where = [jax.random.randint(jax.random.fold_in(key, axis), (), 0, length) for axis, length in enumerate(array.shape)]
        where[longest] = (where[longest] + shift) % array.shape[longest]
        spots.append(tuple(where))
    return array.at[spots[0]].set(low).at[spots[1]].set(largest)


def choose_distinct(own_key, rows, number_of, top, lift):
    ranking = jax.random.permutation(jax.random.fold_in(own_key, 1), number_of)
    favour = ranking
    for power in range(3):
        favour = favour * favour // number_of
    favour = favour * lift // number_of
    lots = jax.random.randint(jax.random.fold_in(own_key, 2), (rows, number_of), 0, 4096) + favour
    holders = jax.random.permutation(jax.random.fold_in(own_key, 3), rows)[jnp.arange(number_of) % rows]
    lots = jnp.where(jnp.arange(rows)[:, None] == holders[None, :], 1 << 14, lots)
    priority = lots * number_of + jnp.arange(number_of)
    return lax.top_k(priority.astype(jnp.int32), top)[1].astype(jnp.int32)


def setup_inputs(seed: int = 0) -> dict:
    seeds = jax.random.split(jax.random.key(seed), 7)
    return {
        "codes": with_ends(jax.random.randint(seeds[0], (ROWS, COVARS), 0, BINS), jax.random.fold_in(seeds[0], 1), 0, BINS - 1).astype(jnp.int32),
        "node": with_ends(jax.random.randint(seeds[1], (ROWS,), 0, NODES), jax.random.fold_in(seeds[1], 1), 0, NODES - 1).astype(jnp.int32),
        "chosen": choose_distinct(seeds[2], NODES, COVARS, SLOTS, 0),
        "arm": with_ends((jax.random.randint(seeds[3], (ROWS,), 0, 2) < 1).astype(jnp.int32), jax.random.fold_in(seeds[3], 1), 0, 1),
        "honest": with_ends((jax.random.randint(seeds[4], (ROWS,), 0, 2) < 1).astype(jnp.int32), jax.random.fold_in(seeds[4], 1), 0, 1),
        "outcome": draw_outcome(jax.random.fold_in(seeds[6], 71), 0),
    }


def split_gain(left_sums, right_sums, weeks):
    def effect_of(sums):
        treated = sums[..., :weeks] / (sums[..., 2 * weeks:2 * weeks + 1] + 1.0)
        control = sums[..., weeks:2 * weeks] / (sums[..., 2 * weeks + 1:2 * weeks + 2] + 1.0)
        return treated - control

    spread_gap = effect_of(left_sums) - effect_of(right_sums)
    left_n = left_sums[..., 2 * weeks] + left_sums[..., 2 * weeks + 1]
    right_n = right_sums[..., 2 * weeks] + right_sums[..., 2 * weeks + 1]
    balance = left_n * right_n / ((left_n + right_n + 1.0) * (left_n + right_n + 1.0))
    return balance * jnp.sum(spread_gap * spread_gap, axis=-1)


def reference(codes, node, chosen, arm, honest, outcome):
    outcome_f = outcome.astype(jnp.float32)
    arm_f = arm.astype(jnp.float32)
    honest_f = honest.astype(jnp.float32)
    treated = honest_f * arm_f
    control = honest_f * (1.0 - arm_f)
    stat_cols = jnp.concatenate([outcome_f * treated[:, None], outcome_f * control[:, None], treated[:, None], control[:, None]], axis=1)
    picked = jnp.take_along_axis(codes, chosen[node], axis=1)
    row_keys = (node[:, None] * BINS + picked).astype(jnp.int32)

    def histogram(column):
        return jax.ops.segment_sum(stat_cols, column, num_segments=NODES * BINS)

    hist = lax.map(histogram, row_keys.T)
    hist = hist.reshape(SLOTS, NODES, BINS, 2 * WEEKS + 2)
    left_sums = jnp.cumsum(hist, axis=2)
    right_sums = left_sums[:, :, -1:, :] - left_sums
    gains = split_gain(left_sums, right_sums, WEEKS)
    best_gain = jnp.max(gains, axis=(0, 2))
    kept = 1.0 - honest_f
    node_hot = (node[:, None] == jnp.arange(NODES, dtype=jnp.int32)[None, :]).astype(jnp.float32)
    est_cols = jnp.concatenate([outcome_f * (kept * arm_f)[:, None], outcome_f * (kept * (1.0 - arm_f))[:, None]], axis=1)
    est_sums = jnp.dot(node_hot.T, est_cols, precision=lax.Precision.HIGHEST)
    est_counts = jnp.dot(node_hot.T, jnp.stack([kept * arm_f, kept * (1.0 - arm_f)], axis=1), precision=lax.Precision.HIGHEST)
    effect = est_sums[:, :WEEKS] / (est_counts[:, 0:1] + 1.0) - est_sums[:, WEEKS:] / (est_counts[:, 1:2] + 1.0)
    return gains, best_gain, effect
```

```python
import jax
import jax.numpy as jnp
from jax import lax
from jax.experimental import pallas as pl
from jax.experimental.pallas import tpu as pltpu
from jax.sharding import PartitionSpec as P

NODES = 16
SLOTS = 32
COVARS = 64
BINS = 256
NX = 4
NZ = 8
NROW = NX * NZ
NPER = 8
UNITS = 256
WEEKS = 16
MESH = pl.DeviceIdType.MESH
F32 = jnp.float32
BF16 = jnp.bfloat16


def row_peer(me, step):
    group, dx = step // NX, step % NX
    dz = ((group + 1) // 2) * (2 * (group % 2) - 1)
    x, z = me // NZ, me % NZ
    return ((x + dx) % NX) * NZ + (z + dz + NZ) % NZ


def kernel(
    codes_ref,
    node_ref,
    chosen_ref,
    arm_ref,
    honest_ref,
    outcome_ref,
    gains_ref,
    best_ref,
    effect_ref,
    obuf,
    mbuf,
    msend,
    left,
    est,
    parts,
    tops,
    o_send,
    o_recv,
    m_send,
    m_recv,
    p_send,
    p_recv,
    t_send,
    t_recv,
):
    me = lax.axis_index("row")
    per = lax.axis_index("period")

    barrier = pltpu.get_barrier_semaphore()

    def greet(step, carry):
        pl.semaphore_signal(
            barrier, inc=1, device_id={"row": row_peer(me, step)}, device_id_type=MESH
        )
        return carry

    lax.fori_loop(1, NROW, greet, 0)

    def greet_period(step, carry):
        pl.semaphore_signal(
            barrier, inc=1, device_id={"period": (per + step) % NPER}, device_id_type=MESH
        )
        return carry

    lax.fori_loop(1, NPER, greet_period, 0)

    node_row = node_ref[...].astype(F32)
    chosen_t = chosen_ref[...].astype(F32).T
    covar = lax.broadcasted_iota(jnp.int32, (SLOTS, COVARS), 1).astype(F32)
    picks = jnp.concatenate(
        [(chosen_t[:, n : n + 1] == covar).astype(F32) for n in range(NODES)], axis=0
    ).astype(BF16)
    by_node = jnp.dot(picks, codes_ref[...].astype(F32).astype(BF16), preferred_element_type=F32)
    picked = jnp.zeros((SLOTS, UNITS), F32)
    for n in range(NODES):
        picked = jnp.where(node_row == n, by_node[n * SLOTS : (n + 1) * SLOTS], picked)
    meta = jnp.concatenate(
        [node_row, arm_ref[...].astype(F32), honest_ref[...].astype(F32)], axis=0
    )
    for s in range(SLOTS):
        msend[s] = jnp.concatenate([picked[s : s + 1], meta], axis=0).astype(BF16)
    obuf[me] = outcome_ref[...]
    mbuf[me] = msend[me]

    pl.semaphore_wait(barrier, NROW - 1 + NPER - 1)

    def outcome_copy(peer, slot):
        return pltpu.make_async_remote_copy(
            src_ref=outcome_ref,
            dst_ref=obuf.at[me],
            send_sem=o_send.at[slot],
            recv_sem=o_recv.at[me],
            device_id={"row": peer},
            device_id_type=MESH,
        )

    def meta_copy(peer, slot):
        return pltpu.make_async_remote_copy(
            src_ref=msend.at[peer],
            dst_ref=mbuf.at[me],
            send_sem=m_send.at[slot],
            recv_sem=m_recv.at[me],
            device_id={"row": peer},
            device_id_type=MESH,
        )

    def send_rows(step, carry):
        peer = row_peer(me, step)
        meta_copy(peer, step).start()
        outcome_copy(peer, step).start()
        return carry

    lax.fori_loop(1, NROW, send_rows, 0)

    def arrived(peer):
        pltpu.make_async_remote_copy(
            src_ref=msend.at[peer],
            dst_ref=mbuf.at[peer],
            send_sem=m_send.at[0],
            recv_sem=m_recv.at[peer],
            device_id={"row": peer},
            device_id_type=MESH,
        ).wait_recv()
        pltpu.make_async_remote_copy(
            src_ref=outcome_ref,
            dst_ref=obuf.at[peer],
            send_sem=o_send.at[0],
            recv_sem=o_recv.at[peer],
            device_id={"row": peer},
            device_id_type=MESH,
        ).wait_recv()

    span = NX * UNITS
    bin_of = lax.broadcasted_iota(jnp.int32, (BINS, span), 0).astype(F32)
    node_of = lax.broadcasted_iota(jnp.int32, (NODES, span), 0).astype(F32)
    left[...] = jnp.zeros_like(left)
    est[...] = jnp.zeros_like(est)

    def one_hot(hit):
        return jnp.where(hit, 1.0, 0.0)

    def gather_group(group, carry):
        rows, metas = [], []
        for dx in range(NX):
            peer = row_peer(me, group * NX + dx)
            if dx == 0:

                @pl.when(group > 0)
                def _():
                    arrived(peer)

            else:
                arrived(peer)
            rows.append(obuf[peer])
            metas.append(mbuf[peer].astype(F32))
        y = jnp.concatenate(rows, axis=1).astype(F32)
        info = jnp.concatenate(metas, axis=1)
        pick, node, arm, honest = (info[k : k + 1] for k in range(4))
        away = jnp.full_like(node, float(NODES))
        in_t = jnp.where((arm * honest) > 0.0, node, away)
        in_c = jnp.where(((1.0 - arm) * honest) > 0.0, node, away)
        kept_t = jnp.where((arm * (1.0 - honest)) > 0.0, node, away)
        kept_c = jnp.where(((1.0 - arm) * (1.0 - honest)) > 0.0, node, away)
        mask = one_hot(pick <= bin_of).astype(BF16)
        wide = jnp.concatenate(
            [jnp.where(in_t == n, y, 0.0).astype(BF16) for n in range(NODES)]
            + [jnp.where(in_c == n, y, 0.0).astype(BF16) for n in range(NODES)]
            + [one_hot(in_t == node_of).astype(BF16), one_hot(in_c == node_of).astype(BF16)],
            axis=0,
        )
        left[...] += lax.dot_general(
            wide, mask, (((1,), (1,)), ((), ())), preferred_element_type=F32
        )
        kept = jnp.concatenate(
            [one_hot(kept_t == node_of).astype(BF16), one_hot(kept_c == node_of).astype(BF16)],
            axis=0,
        )
        stats = jnp.concatenate([y.astype(BF16), jnp.ones((16, span), BF16)], axis=0)
        est[...] += lax.dot_general(
            kept, stats, (((1,), (1,)), ((), ())), preferred_element_type=F32
        )
        return carry

    lax.fori_loop(0, NZ, gather_group, 0)

    half = NODES * WEEKS
    count_t = left[2 * half : 2 * half + NODES, :]
    count_c = left[2 * half + NODES :, :]
    rest_t = count_t[:, BINS - 1 :] - count_t
    rest_c = count_c[:, BINS - 1 :] - count_c
    w_lt = 1.0 / (count_t + 1.0)
    w_lc = 1.0 / (count_c + 1.0)
    w_rt = 1.0 / (rest_t + 1.0)
    w_rc = 1.0 / (rest_c + 1.0)
    sums = []
    for n in range(NODES):
        lt = left[n * WEEKS : (n + 1) * WEEKS, :]
        lc = left[half + n * WEEKS : half + (n + 1) * WEEKS, :]
        rt = lt[:, BINS - 1 :] - lt
        rc = lc[:, BINS - 1 :] - lc
        gap = (lt * w_lt[n : n + 1] - lc * w_lc[n : n + 1]) - (
            rt * w_rt[n : n + 1] - rc * w_rc[n : n + 1]
        )
        sums.append(jnp.sum(gap * gap, axis=0, keepdims=True))
    parts[per] = jnp.concatenate(sums, axis=0)

    def part_copy(step):
        other = (per + step) % NPER
        return pltpu.make_async_remote_copy(
            src_ref=parts.at[per],
            dst_ref=parts.at[per],
            send_sem=p_send.at[step],
            recv_sem=p_recv.at[per],
            device_id={"period": other},
            device_id_type=MESH,
        )

    for step in range(1, NPER):
        part_copy(step).start()

    effect_ref[...] = est[:NODES, :WEEKS] / (est[:NODES, WEEKS : WEEKS + 1] + 1.0) - est[
        NODES:, :WEEKS
    ] / (est[NODES:, WEEKS : WEEKS + 1] + 1.0)
    n_l = count_t + count_c
    n_r = rest_t + rest_c
    balance = n_l * n_r / ((n_l + n_r + 1.0) * (n_l + n_r + 1.0))

    for step in range(1, NPER):
        other = (per + step) % NPER
        pltpu.make_async_remote_copy(
            src_ref=parts.at[other],
            dst_ref=parts.at[other],
            send_sem=p_send.at[step],
            recv_sem=p_recv.at[other],
            device_id={"period": other},
            device_id_type=MESH,
        ).wait_recv()
    spread = parts[0]
    for p in range(1, NPER):
        spread = spread + parts[p]
    full = balance * spread

    peak = jnp.max(full, axis=1, keepdims=True)
    diag = lax.broadcasted_iota(jnp.int32, (NODES, 128), 0) == lax.broadcasted_iota(
        jnp.int32, (NODES, 128), 1
    )
    tops[me] = jnp.sum(jnp.where(diag, peak, 0.0), axis=0, keepdims=True)

    def top_copy(peer, slot):
        return pltpu.make_async_remote_copy(
            src_ref=tops.at[me],
            dst_ref=tops.at[me],
            send_sem=t_send.at[slot],
            recv_sem=t_recv.at[me],
            device_id={"row": peer},
            device_id_type=MESH,
        )

    def send_tops(step, carry):
        top_copy(row_peer(me, step), step).start()
        return carry

    lax.fori_loop(1, NROW, send_tops, 0)

    share = BINS // NPER
    mine = jnp.zeros((NODES, share), F32)
    for p in range(NPER):
        mine = jnp.where(per == p, full[:, p * share : (p + 1) * share], mine)
    gains_ref[...] = mine

    def top_wait(step, carry):
        peer = row_peer(me, step)
        pltpu.make_async_remote_copy(
            src_ref=tops.at[peer],
            dst_ref=tops.at[peer],
            send_sem=t_send.at[step],
            recv_sem=t_recv.at[peer],
            device_id={"row": peer},
            device_id_type=MESH,
        ).wait_recv()
        return carry

    lax.fori_loop(1, NROW, top_wait, 0)
    best_ref[...] = jnp.max(tops[...], axis=0)[:, :NODES]

    def drain(step, carry):
        peer = row_peer(me, step)
        meta_copy(peer, step).wait_send()
        outcome_copy(peer, step).wait_send()
        top_copy(peer, step).wait_send()
        return carry

    lax.fori_loop(1, NROW, drain, 0)
    for step in range(1, NPER):
        part_copy(step).wait_send()


def shards(codes, node, chosen, arm, honest, outcome):
    vmem = pl.BlockSpec(memory_space=pltpu.VMEM)
    dma = pltpu.SemaphoreType.DMA
    gains, best, effect = pl.pallas_call(
        kernel,
        out_shape=(
            jax.ShapeDtypeStruct((NODES, BINS // NPER), F32),
            jax.ShapeDtypeStruct((1, NODES), F32),
            jax.ShapeDtypeStruct((NODES, WEEKS), F32),
        ),
        in_specs=[vmem] * 6,
        out_specs=(vmem,) * 3,
        scratch_shapes=[
            pltpu.VMEM((NROW, WEEKS, UNITS), BF16),
            pltpu.VMEM((NROW, 4, UNITS), BF16),
            pltpu.VMEM((NROW, 4, UNITS), BF16),
            pltpu.VMEM((2 * NODES * WEEKS + 2 * NODES, BINS), F32),
            pltpu.VMEM((2 * NODES, 32), F32),
            pltpu.VMEM((NPER, NODES, BINS), F32),
            pltpu.VMEM((NROW, 1, 128), F32),
            dma((NROW,)),
            dma((NROW,)),
            dma((NROW,)),
            dma((NROW,)),
            dma((NPER,)),
            dma((NPER,)),
            dma((NROW,)),
            dma((NROW,)),
        ],
        compiler_params=pltpu.CompilerParams(collective_id=0, has_side_effects=True),
        name="level",
    )(
        codes.T,
        node.reshape(1, UNITS),
        chosen,
        arm.reshape(1, UNITS),
        honest.reshape(1, UNITS),
        outcome.T,
    )
    return gains[None], best.reshape(NODES), effect


def solution(mesh):
    in_specs = (P("row", None), P("row"), P(), P("row"), P("row"), P("row", "period"))
    out_specs = (P("row", None, "period"), P(), P(None, "period"))
    return jax.shard_map(shards, mesh=mesh, in_specs=in_specs, out_specs=out_specs, check_vma=False)
```

```python
import jax
import jax.numpy as jnp
from jax import lax
from jax.experimental import pallas as pl
from jax.experimental.pallas import tpu as pltpu
from jax.sharding import PartitionSpec as P

NODES = 16
SLOTS = 32
COVARS = 64
BINS = 256
NX = 4
NZ = 8
NROW = NX * NZ
NPER = 8
UNITS = 256
WEEKS = 16
HALF = NODES * WEEKS
MESH = pl.DeviceIdType.MESH
F32 = jnp.float32
BF16 = jnp.bfloat16
Z_SEND = (4, 3, -3, 2, -2, 1, -1)
Z_TAKE = (0, 1, -1, 2, -2, 3, -3, 4)
X_SEND = (2, 1, 3)
P_SEND = (4, 5, 3, 2, 6, 7, 1)


def kernel(
    codes_hbm,
    node_hbm,
    chosen_hbm,
    arm_hbm,
    honest_hbm,
    outcome_hbm,
    gains_ref,
    best_ref,
    effect_ref,
    codes_ref,
    node_ref,
    chosen_ref,
    arm_ref,
    honest_ref,
    obuf,
    msend,
    mzbuf,
    mxbuf,
    left,
    est,
    parts,
    tops,
    in_sem,
    zo_send,
    zm_send,
    xo_send,
    xm_send,
    o_recv,
    mz_recv,
    mx_recv,
    p_send,
    p_recv,
    t_send,
    t_recv,
):
    me = lax.axis_index("row")
    per = lax.axis_index("period")
    my_x = lax.div(me, NZ)
    my_z = lax.rem(me, NZ)
    z_at = {dz: lax.rem(my_z + (dz + NZ), NZ) for dz in Z_TAKE}
    x_at = {dx: lax.rem(my_x + dx, NX) for dx in range(NX)}

    def row_of(dx, dz):
        return x_at[dx] * NZ + z_at[dz]

    barrier = pltpu.get_barrier_semaphore()
    for dz in Z_SEND:
        pl.semaphore_signal(
            barrier, inc=1, device_id={"row": row_of(0, dz)}, device_id_type=MESH
        )
    for dx in X_SEND:
        pl.semaphore_signal(
            barrier, inc=1, device_id={"row": row_of(dx, 0)}, device_id_type=MESH
        )
    for dp in P_SEND:
        pl.semaphore_signal(
            barrier, inc=1, device_id={"period": lax.rem(per + dp, NPER)}, device_id_type=MESH
        )

    loads = [
        pltpu.make_async_copy(src, dst, in_sem.at[k])
        for k, (src, dst) in enumerate(
            [
                (codes_hbm, codes_ref),
                (node_hbm, node_ref),
                (chosen_hbm, chosen_ref),
                (arm_hbm, arm_ref),
                (honest_hbm, honest_ref),
                (outcome_hbm, obuf.at[me]),
            ]
        )
    ]
    for load in loads:
        load.start()
    for load in loads:
        load.wait()

    node_row = node_ref[...].astype(F32)
    chosen_t = chosen_ref[...].astype(F32).T
    covar = lax.broadcasted_iota(jnp.int32, (SLOTS, COVARS), 1).astype(F32)
    picks = jnp.concatenate(
        [jnp.where(chosen_t[:, n : n + 1] == covar, 1.0, 0.0) for n in range(NODES)], axis=0
    ).astype(BF16)
    by_node = jnp.dot(picks, codes_ref[...].astype(F32).astype(BF16), preferred_element_type=F32)
    picked = jnp.zeros((SLOTS, UNITS), F32)
    for n in range(NODES):
        picked = jnp.where(node_row == n, by_node[n * SLOTS : (n + 1) * SLOTS], picked)
    meta = jnp.concatenate(
        [node_row, arm_ref[...].astype(F32), honest_ref[...].astype(F32)], axis=0
    )
    for s in range(SLOTS):
        msend[s % NZ, s // NZ] = jnp.concatenate([picked[s : s + 1], meta], axis=0).astype(BF16)

    pl.semaphore_wait(barrier, len(Z_SEND) + len(X_SEND) + len(P_SEND))

    def outcome_to_z(dz):
        return pltpu.make_async_remote_copy(
            src_ref=obuf.at[me],
            dst_ref=obuf.at[me],
            send_sem=zo_send.at[dz % NZ],
            recv_sem=o_recv.at[me],
            device_id={"row": row_of(0, dz)},
            device_id_type=MESH,
        )

    def meta_to_z(dz):
        return pltpu.make_async_remote_copy(
            src_ref=msend.at[z_at[dz]],
            dst_ref=mzbuf.at[my_z],
            send_sem=zm_send.at[dz % NZ],
            recv_sem=mz_recv.at[my_z],
            device_id={"row": row_of(0, dz)},
            device_id_type=MESH,
        )

    def outcome_to_x(dz, dx):
        row = row_of(0, dz)
        return pltpu.make_async_remote_copy(
            src_ref=obuf.at[row],
            dst_ref=obuf.at[row],
            send_sem=xo_send.at[(dz % NZ) * NX + dx],
            recv_sem=o_recv.at[row],
            device_id={"row": row_of(dx, 0)},
            device_id_type=MESH,
        )

    def meta_to_x(dz, dx):
        row = row_of(0, dz)
        source = msend.at[my_z] if dz == 0 else mzbuf.at[z_at[dz]]
        return pltpu.make_async_remote_copy(
            src_ref=source.at[x_at[dx]],
            dst_ref=mxbuf.at[row],
            send_sem=xm_send.at[(dz % NZ) * NX + dx],
            recv_sem=mx_recv.at[row],
            device_id={"row": row_of(dx, 0)},
            device_id_type=MESH,
        )

    def outcome_arrived(row):
        pltpu.make_async_remote_copy(
            src_ref=obuf.at[row],
            dst_ref=obuf.at[row],
            send_sem=zo_send.at[0],
            recv_sem=o_recv.at[row],
            device_id={"row": row},
            device_id_type=MESH,
        ).wait_recv()

    for dz in Z_SEND:
        meta_to_z(dz).start()
        outcome_to_z(dz).start()
    for dx in X_SEND:
        meta_to_x(0, dx).start()
        outcome_to_x(0, dx).start()

    left[...] = jnp.zeros_like(left)
    mxbuf[me] = msend[my_z, my_x]
    for dz in Z_TAKE[1:]:
        row = row_of(0, dz)
        pltpu.make_async_remote_copy(
            src_ref=mzbuf.at[z_at[dz]],
            dst_ref=mzbuf.at[z_at[dz]],
            send_sem=zm_send.at[0],
            recv_sem=mz_recv.at[z_at[dz]],
            device_id={"row": row},
            device_id_type=MESH,
        ).wait_recv()
        for dx in X_SEND:
            meta_to_x(dz, dx).start()
        outcome_arrived(row)
        for dx in X_SEND:
            outcome_to_x(dz, dx).start()
        mxbuf[row] = mzbuf[z_at[dz], my_x]

    def load_rows(rows):
        y = jnp.concatenate([obuf[row] for row in rows], axis=1)
        info = jnp.concatenate([mxbuf[row].astype(F32) for row in rows], axis=1)
        return y, [info[k : k + 1] for k in range(4)]

    def spread(row):
        return jnp.broadcast_to(row, (NODES, row.shape[1])).astype(BF16)

    def add_rows(rows):
        y, (pick, node, arm, honest) = load_rows(rows)
        span = y.shape[1]
        away = jnp.full_like(node, float(NODES))
        in_t = spread(jnp.where((arm * honest) > 0.0, node, away))
        in_c = spread(jnp.where(((1.0 - arm) * honest) > 0.0, node, away))
        pick = spread(pick)
        lane = lax.broadcasted_iota(jnp.int32, (NODES, span), 0).astype(F32).astype(BF16)
        one = jnp.ones((NODES, span), BF16)
        zero = jnp.zeros((NODES, span), BF16)
        mask = jnp.concatenate(
            [
                jnp.where(pick <= lane + jnp.asarray(float(k * NODES), BF16), one, zero)
                for k in range(BINS // NODES)
            ],
            axis=0,
        )
        wide = jnp.concatenate(
            [jnp.where(in_t == jnp.asarray(float(n), BF16), y, zero) for n in range(NODES)]
            + [jnp.where(in_c == jnp.asarray(float(n), BF16), y, zero) for n in range(NODES)]
            + [jnp.where(in_t == lane, one, zero), jnp.where(in_c == lane, one, zero)],
            axis=0,
        )
        left[...] += lax.dot_general(
            wide, mask, (((1,), (1,)), ((), ())), preferred_element_type=F32
        )

    add_rows([row_of(0, dz) for dz in Z_TAKE])

    def take_pair(pair, carry):
        rows = []
        for k in range(2):
            step = pair * 2 + k
            dz = ((step + 1) // 2) * (2 * (step % 2) - 1)
            z = lax.rem(my_z + dz + NZ, NZ)
            for dx in X_SEND:
                row = x_at[dx] * NZ + z
                pltpu.make_async_remote_copy(
                    src_ref=mxbuf.at[row],
                    dst_ref=mxbuf.at[row],
                    send_sem=zm_send.at[0],
                    recv_sem=mx_recv.at[row],
                    device_id={"row": row},
                    device_id_type=MESH,
                ).wait_recv()
                outcome_arrived(row)
                rows.append(row)
        add_rows(rows)
        return carry

    lax.fori_loop(0, NZ // 2, take_pair, 0)

    count_t = left[2 * HALF : 2 * HALF + NODES, :]
    count_c = left[2 * HALF + NODES :, :]
    rest_t = count_t[:, BINS - 1 :] - count_t
    rest_c = count_c[:, BINS - 1 :] - count_c
    w_lt = 1.0 / (count_t + 1.0)
    w_lc = 1.0 / (count_c + 1.0)
    w_rt = 1.0 / (rest_t + 1.0)
    w_rc = 1.0 / (rest_c + 1.0)

    def part_copy(chunk, dp, owner):
        return pltpu.make_async_remote_copy(
            src_ref=parts.at[chunk, owner],
            dst_ref=parts.at[chunk, owner],
            send_sem=p_send.at[chunk * NPER + dp],
            recv_sem=p_recv.at[chunk * NPER + owner],
            device_id={"period": lax.rem(per + dp, NPER)},
            device_id_type=MESH,
        )

    for chunk in range(2):
        sums = []
        for n in range(chunk * 8, chunk * 8 + 8):
            lt = left[n * WEEKS : (n + 1) * WEEKS, :]
            lc = left[HALF + n * WEEKS : HALF + (n + 1) * WEEKS, :]
            rt = lt[:, BINS - 1 :] - lt
            rc = lc[:, BINS - 1 :] - lc
            gap = (lt * w_lt[n : n + 1] - lc * w_lc[n : n + 1]) - (
                rt * w_rt[n : n + 1] - rc * w_rc[n : n + 1]
            )
            sums.append(jnp.sum(gap * gap, axis=0, keepdims=True))
        parts[chunk, per] = jnp.concatenate(sums, axis=0)
        for dp in P_SEND:
            part_copy(chunk, dp, per).start()

    est[...] = jnp.zeros_like(est)

    def add_kept(z, carry):
        y, (_, node, arm, honest) = load_rows([x * NZ + z for x in range(NX)])
        span = y.shape[1]
        away = jnp.full_like(node, float(NODES))
        kept_t = spread(jnp.where((arm * (1.0 - honest)) > 0.0, node, away))
        kept_c = spread(jnp.where(((1.0 - arm) * (1.0 - honest)) > 0.0, node, away))
        lane = lax.broadcasted_iota(jnp.int32, (NODES, span), 0).astype(F32).astype(BF16)
        one = jnp.ones((NODES, span), BF16)
        zero = jnp.zeros((NODES, span), BF16)
        kept = jnp.concatenate(
            [jnp.where(kept_t == lane, one, zero), jnp.where(kept_c == lane, one, zero)], axis=0
        )
        est[...] += lax.dot_general(
            kept,
            jnp.concatenate([y, one], axis=0),
            (((1,), (1,)), ((), ())),
            preferred_element_type=F32,
        )
        return carry

    lax.fori_loop(0, NZ, add_kept, 0)
    effect_ref[...] = est[:NODES, :WEEKS] / (est[:NODES, WEEKS : WEEKS + 1] + 1.0) - est[
        NODES:, :WEEKS
    ] / (est[NODES:, WEEKS : WEEKS + 1] + 1.0)
    n_l = count_t + count_c
    n_r = rest_t + rest_c
    balance = n_l * n_r / ((n_l + n_r + 1.0) * (n_l + n_r + 1.0))

    spreads = []
    for chunk in range(2):
        for dp in P_SEND:
            part_copy(chunk, dp, lax.rem(per + dp, NPER)).wait_recv()
        total = parts[chunk, 0]
        for p in range(1, NPER):
            total = total + parts[chunk, p]
        spreads.append(total)
    full = balance * jnp.concatenate(spreads, axis=0)

    peak = jnp.max(full, axis=1, keepdims=True)
    diag = lax.broadcasted_iota(jnp.int32, (NODES, 128), 0) == lax.broadcasted_iota(
        jnp.int32, (NODES, 128), 1
    )
    tops[me] = jnp.sum(jnp.where(diag, peak, 0.0), axis=0, keepdims=True)

    far_first = sorted(
        ((dx, dz) for dx in range(NX) for dz in Z_TAKE if dx or dz),
        key=lambda d: -(min(d[0], NX - d[0]) + abs(d[1])),
    )

    def top_copy(dx, dz, owner):
        return pltpu.make_async_remote_copy(
            src_ref=tops.at[owner],
            dst_ref=tops.at[owner],
            send_sem=t_send.at[dx * NZ + dz % NZ],
            recv_sem=t_recv.at[owner],
            device_id={"row": row_of(dx, dz)},
            device_id_type=MESH,
        )

    for dx, dz in far_first:
        top_copy(dx, dz, me).start()

    share = BINS // NPER
    mine = jnp.zeros((NODES, share), F32)
    for p in range(NPER):
        mine = jnp.where(per == p, full[:, p * share : (p + 1) * share], mine)
    gains_ref[...] = mine

    for dz in Z_SEND:
        meta_to_z(dz).wait_send()
        outcome_to_z(dz).wait_send()
    for dz in Z_TAKE:
        for dx in X_SEND:
            meta_to_x(dz, dx).wait_send()
            outcome_to_x(dz, dx).wait_send()
    for chunk in range(2):
        for dp in P_SEND:
            part_copy(chunk, dp, per).wait_send()

    for dx, dz in far_first:
        top_copy(dx, dz, row_of(dx, dz)).wait_recv()
    best_ref[...] = jnp.max(tops[...], axis=0)[:, :NODES]
    for dx, dz in far_first:
        top_copy(dx, dz, me).wait_send()


def shards(codes, node, chosen, arm, honest, outcome):
    vmem = pl.BlockSpec(memory_space=pltpu.VMEM)
    hbm = pl.BlockSpec(memory_space=pl.ANY)
    dma = pltpu.SemaphoreType.DMA
    gains, best, effect = pl.pallas_call(
        kernel,
        out_shape=(
            jax.ShapeDtypeStruct((NODES, BINS // NPER), F32),
            jax.ShapeDtypeStruct((1, NODES), F32),
            jax.ShapeDtypeStruct((NODES, WEEKS), F32),
        ),
        in_specs=[hbm] * 6,
        out_specs=(vmem,) * 3,
        scratch_shapes=[
            pltpu.VMEM((COVARS, UNITS), jnp.int32),
            pltpu.VMEM((1, UNITS), jnp.int32),
            pltpu.VMEM((NODES, SLOTS), jnp.int32),
            pltpu.VMEM((1, UNITS), jnp.int32),
            pltpu.VMEM((1, UNITS), jnp.int32),
            pltpu.VMEM((NROW, WEEKS, UNITS), BF16),
            pltpu.VMEM((NZ, NX, 4, UNITS), BF16),
            pltpu.VMEM((NZ, NX, 4, UNITS), BF16),
            pltpu.VMEM((NROW, 4, UNITS), BF16),
            pltpu.VMEM((2 * HALF + 2 * NODES, BINS), F32),
            pltpu.VMEM((2 * NODES, 2 * WEEKS), F32),
            pltpu.VMEM((2, NPER, 8, BINS), F32),
            pltpu.VMEM((NROW, 1, 128), F32),
            dma((6,)),
            dma((NZ,)),
            dma((NZ,)),
            dma((NROW,)),
            dma((NROW,)),
            dma((NROW,)),
            dma((NZ,)),
            dma((NROW,)),
            dma((2 * NPER,)),
            dma((2 * NPER,)),
            dma((NROW,)),
            dma((NROW,)),
        ],
        compiler_params=pltpu.CompilerParams(collective_id=0, has_side_effects=True),
        name="level",
    )(
        codes.T,
        node.reshape(1, UNITS),
        chosen,
        arm.reshape(1, UNITS),
        honest.reshape(1, UNITS),
        outcome.T,
    )
    return gains[None], best.reshape(NODES), effect


def solution(mesh):
    in_specs = (P("row", None), P("row"), P(), P("row"), P("row"), P("row", "period"))
    out_specs = (P("row", None, "period"), P(), P(None, "period"))
    return jax.shard_map(shards, mesh=mesh, in_specs=in_specs, out_specs=out_specs, check_vma=False)
```

```python
import jax
import jax.numpy as jnp
from jax import lax
from jax.experimental import pallas as pl
from jax.experimental.pallas import tpu as pltpu
from jax.sharding import PartitionSpec as P

NODES = 16
SLOTS = 32
COVARS = 64
BINS = 256
NX = 4
NZ = 8
NROW = NX * NZ
NPER = 8
UNITS = 256
WEEKS = 16
HALF = NODES * WEEKS
MESH = pl.DeviceIdType.MESH
F32 = jnp.float32
BF16 = jnp.bfloat16
Z_SEND = (4, 3, -3, 2, -2, 1, -1)
Z_TAKE = (0, 1, -1, 2, -2, 3, -3, 4)
X_SEND = (2, 1, 3)
P_SEND = (4, 5, 3, 2, 6, 7, 1)


def kernel(
    codes_hbm,
    node_hbm,
    chosen_hbm,
    arm_hbm,
    honest_hbm,
    outcome_hbm,
    packed_ref,
    codes_ref,
    node_ref,
    chosen_ref,
    arm_ref,
    honest_ref,
    obuf,
    msend,
    mzbuf,
    mxbuf,
    left,
    est,
    parts,
    tops,
    in_sem,
    zo_send,
    zm_send,
    xo_send,
    xm_send,
    o_recv,
    mz_recv,
    mx_recv,
    p_send,
    p_recv,
    t_send,
    t_recv,
):
    me = lax.axis_index("row")
    per = lax.axis_index("period")
    my_x = lax.div(me, NZ)
    my_z = lax.rem(me, NZ)
    z_at = {dz: lax.rem(my_z + (dz + NZ), NZ) for dz in Z_TAKE}
    x_at = {dx: lax.rem(my_x + dx, NX) for dx in range(NX)}

    def row_of(dx, dz):
        return x_at[dx] * NZ + z_at[dz]

    barrier = pltpu.get_barrier_semaphore()
    for dz in Z_SEND:
        pl.semaphore_signal(
            barrier, inc=1, device_id={"row": row_of(0, dz)}, device_id_type=MESH
        )
    for dx in X_SEND:
        pl.semaphore_signal(
            barrier, inc=1, device_id={"row": row_of(dx, 0)}, device_id_type=MESH
        )
    for dp in P_SEND:
        pl.semaphore_signal(
            barrier, inc=1, device_id={"period": lax.rem(per + dp, NPER)}, device_id_type=MESH
        )

    loads = [
        pltpu.make_async_copy(src, dst, in_sem.at[k])
        for k, (src, dst) in enumerate(
            [
                (codes_hbm, codes_ref),
                (node_hbm, node_ref),
                (chosen_hbm, chosen_ref),
                (arm_hbm, arm_ref),
                (honest_hbm, honest_ref),
                (outcome_hbm, obuf.at[me]),
            ]
        )
    ]
    for load in loads:
        load.start()
    for load in loads:
        load.wait()

    node_row = node_ref[...].astype(F32)
    chosen_t = chosen_ref[...].astype(F32).T
    covar = lax.broadcasted_iota(jnp.int32, (SLOTS, COVARS), 1).astype(F32)
    picks = jnp.concatenate(
        [jnp.where(chosen_t[:, n : n + 1] == covar, 1.0, 0.0) for n in range(NODES)], axis=0
    ).astype(BF16)
    by_node = jnp.dot(picks, codes_ref[...].astype(F32).astype(BF16), preferred_element_type=F32)
    picked = jnp.zeros((SLOTS, UNITS), F32)
    for n in range(NODES):
        picked = jnp.where(node_row == n, by_node[n * SLOTS : (n + 1) * SLOTS], picked)
    meta = jnp.concatenate(
        [node_row, arm_ref[...].astype(F32), honest_ref[...].astype(F32)], axis=0
    )
    for s in range(SLOTS):
        msend[s % NZ, s // NZ] = jnp.concatenate([picked[s : s + 1], meta], axis=0).astype(BF16)

    pl.semaphore_wait(barrier, len(Z_SEND) + len(X_SEND) + len(P_SEND))

    def outcome_to_z(dz):
        return pltpu.make_async_remote_copy(
            src_ref=obuf.at[me],
            dst_ref=obuf.at[me],
            send_sem=zo_send.at[dz % NZ],
            recv_sem=o_recv.at[me],
            device_id={"row": row_of(0, dz)},
            device_id_type=MESH,
        )

    def meta_to_z(dz):
        return pltpu.make_async_remote_copy(
            src_ref=msend.at[z_at[dz]],
            dst_ref=mzbuf.at[my_z],
            send_sem=zm_send.at[dz % NZ],
            recv_sem=mz_recv.at[my_z],
            device_id={"row": row_of(0, dz)},
            device_id_type=MESH,
        )

    def outcome_to_x(dz, dx):
        row = row_of(0, dz)
        return pltpu.make_async_remote_copy(
            src_ref=obuf.at[row],
            dst_ref=obuf.at[row],
            send_sem=xo_send.at[(dz % NZ) * NX + dx],
            recv_sem=o_recv.at[row],
            device_id={"row": row_of(dx, 0)},
            device_id_type=MESH,
        )

    def meta_to_x(dz, dx):
        row = row_of(0, dz)
        source = msend.at[my_z] if dz == 0 else mzbuf.at[z_at[dz]]
        return pltpu.make_async_remote_copy(
            src_ref=source.at[x_at[dx]],
            dst_ref=mxbuf.at[row],
            send_sem=xm_send.at[(dz % NZ) * NX + dx],
            recv_sem=mx_recv.at[row],
            device_id={"row": row_of(dx, 0)},
            device_id_type=MESH,
        )

    def outcome_arrived(row):
        pltpu.make_async_remote_copy(
            src_ref=obuf.at[row],
            dst_ref=obuf.at[row],
            send_sem=zo_send.at[0],
            recv_sem=o_recv.at[row],
            device_id={"row": row},
            device_id_type=MESH,
        ).wait_recv()

    for dz in Z_SEND:
        meta_to_z(dz).start()
        outcome_to_z(dz).start()
    for dx in X_SEND:
        meta_to_x(0, dx).start()
        outcome_to_x(0, dx).start()

    left[...] = jnp.zeros_like(left)
    packed_ref[...] = jnp.zeros_like(packed_ref)
    mxbuf[me] = msend[my_z, my_x]
    for dz in Z_TAKE[1:]:
        row = row_of(0, dz)
        pltpu.make_async_remote_copy(
            src_ref=mzbuf.at[z_at[dz]],
            dst_ref=mzbuf.at[z_at[dz]],
            send_sem=zm_send.at[0],
            recv_sem=mz_recv.at[z_at[dz]],
            device_id={"row": row},
            device_id_type=MESH,
        ).wait_recv()
        for dx in X_SEND:
            meta_to_x(dz, dx).start()
        outcome_arrived(row)
        for dx in X_SEND:
            outcome_to_x(dz, dx).start()
        mxbuf[row] = mzbuf[z_at[dz], my_x]

    def load_rows(rows):
        y = jnp.concatenate([obuf[row] for row in rows], axis=1)
        info = jnp.concatenate([mxbuf[row].astype(F32) for row in rows], axis=1)
        return y, [info[k : k + 1] for k in range(4)]

    def spread(row):
        return jnp.broadcast_to(row, (NODES, row.shape[1])).astype(BF16)

    def add_rows(rows):
        y, (pick, node, arm, honest) = load_rows(rows)
        span = y.shape[1]
        away = jnp.full_like(node, float(NODES))
        in_t = spread(jnp.where((arm * honest) > 0.0, node, away))
        in_c = spread(jnp.where(((1.0 - arm) * honest) > 0.0, node, away))
        pick = spread(pick)
        lane = lax.broadcasted_iota(jnp.int32, (NODES, span), 0).astype(F32).astype(BF16)
        one = jnp.ones((NODES, span), BF16)
        zero = jnp.zeros((NODES, span), BF16)
        mask = jnp.concatenate(
            [
                jnp.where(pick <= lane + jnp.asarray(float(k * NODES), BF16), one, zero)
                for k in range(BINS // NODES)
            ],
            axis=0,
        )
        wide = jnp.concatenate(
            [jnp.where(in_t == jnp.asarray(float(n), BF16), y, zero) for n in range(NODES)]
            + [jnp.where(in_c == jnp.asarray(float(n), BF16), y, zero) for n in range(NODES)]
            + [jnp.where(in_t == lane, one, zero), jnp.where(in_c == lane, one, zero)],
            axis=0,
        )
        left[...] += lax.dot_general(
            wide, mask, (((1,), (1,)), ((), ())), preferred_element_type=F32
        )

    add_rows([row_of(0, dz) for dz in Z_TAKE])

    def take_pair(pair, carry):
        rows = []
        for k in range(2):
            step = pair * 2 + k
            dz = ((step + 1) // 2) * (2 * (step % 2) - 1)
            z = lax.rem(my_z + dz + NZ, NZ)
            for dx in X_SEND:
                row = x_at[dx] * NZ + z
                pltpu.make_async_remote_copy(
                    src_ref=mxbuf.at[row],
                    dst_ref=mxbuf.at[row],
                    send_sem=zm_send.at[0],
                    recv_sem=mx_recv.at[row],
                    device_id={"row": row},
                    device_id_type=MESH,
                ).wait_recv()
                outcome_arrived(row)
                rows.append(row)
        add_rows(rows)
        return carry

    lax.fori_loop(0, NZ // 2, take_pair, 0)

    count_t = left[2 * HALF : 2 * HALF + NODES, :]
    count_c = left[2 * HALF + NODES :, :]
    rest_t = count_t[:, BINS - 1 :] - count_t
    rest_c = count_c[:, BINS - 1 :] - count_c
    w_lt = 1.0 / (count_t + 1.0)
    w_lc = 1.0 / (count_c + 1.0)
    w_rt = 1.0 / (rest_t + 1.0)
    w_rc = 1.0 / (rest_c + 1.0)

    def part_copy(chunk, dp, owner):
        return pltpu.make_async_remote_copy(
            src_ref=parts.at[chunk, owner],
            dst_ref=parts.at[chunk, owner],
            send_sem=p_send.at[chunk * NPER + dp],
            recv_sem=p_recv.at[chunk * NPER + owner],
            device_id={"period": lax.rem(per + dp, NPER)},
            device_id_type=MESH,
        )

    for chunk in range(2):
        sums = []
        for n in range(chunk * 8, chunk * 8 + 8):
            lt = left[n * WEEKS : (n + 1) * WEEKS, :]
            lc = left[HALF + n * WEEKS : HALF + (n + 1) * WEEKS, :]
            rt = lt[:, BINS - 1 :] - lt
            rc = lc[:, BINS - 1 :] - lc
            gap = (lt * w_lt[n : n + 1] - lc * w_lc[n : n + 1]) - (
                rt * w_rt[n : n + 1] - rc * w_rc[n : n + 1]
            )
            sums.append(jnp.sum(gap * gap, axis=0, keepdims=True))
        parts[chunk, per] = jnp.concatenate(sums, axis=0)
        for dp in P_SEND:
            part_copy(chunk, dp, per).start()

    est[...] = jnp.zeros_like(est)

    def add_kept(z, carry):
        y, (_, node, arm, honest) = load_rows([x * NZ + z for x in range(NX)])
        span = y.shape[1]
        away = jnp.full_like(node, float(NODES))
        kept_t = spread(jnp.where((arm * (1.0 - honest)) > 0.0, node, away))
        kept_c = spread(jnp.where(((1.0 - arm) * (1.0 - honest)) > 0.0, node, away))
        lane = lax.broadcasted_iota(jnp.int32, (NODES, span), 0).astype(F32).astype(BF16)
        one = jnp.ones((NODES, span), BF16)
        zero = jnp.zeros((NODES, span), BF16)
        kept = jnp.concatenate(
            [jnp.where(kept_t == lane, one, zero), jnp.where(kept_c == lane, one, zero)], axis=0
        )
        est[...] += lax.dot_general(
            kept,
            jnp.concatenate([y, one], axis=0),
            (((1,), (1,)), ((), ())),
            preferred_element_type=F32,
        )
        return carry

    lax.fori_loop(0, NZ, add_kept, 0)
    packed_ref[NODES : 2 * NODES, :WEEKS] = est[:NODES, :WEEKS] / (est[:NODES, WEEKS : WEEKS + 1] + 1.0) - est[
        NODES:, :WEEKS
    ] / (est[NODES:, WEEKS : WEEKS + 1] + 1.0)
    n_l = count_t + count_c
    n_r = rest_t + rest_c
    balance = n_l * n_r / ((n_l + n_r + 1.0) * (n_l + n_r + 1.0))

    spreads = []
    for chunk in range(2):
        for dp in P_SEND:
            part_copy(chunk, dp, lax.rem(per + dp, NPER)).wait_recv()
        total = parts[chunk, 0]
        for p in range(1, NPER):
            total = total + parts[chunk, p]
        spreads.append(total)
    full = balance * jnp.concatenate(spreads, axis=0)

    peak = jnp.max(full, axis=1, keepdims=True)
    diag = lax.broadcasted_iota(jnp.int32, (NODES, 128), 0) == lax.broadcasted_iota(
        jnp.int32, (NODES, 128), 1
    )
    tops[me] = jnp.sum(jnp.where(diag, peak, 0.0), axis=0, keepdims=True)

    far_first = sorted(
        ((dx, dz) for dx in range(NX) for dz in Z_TAKE if dx or dz),
        key=lambda d: -(min(d[0], NX - d[0]) + abs(d[1])),
    )

    def top_copy(dx, dz, owner):
        return pltpu.make_async_remote_copy(
            src_ref=tops.at[owner],
            dst_ref=tops.at[owner],
            send_sem=t_send.at[dx * NZ + dz % NZ],
            recv_sem=t_recv.at[owner],
            device_id={"row": row_of(dx, dz)},
            device_id_type=MESH,
        )

    for dx, dz in far_first:
        top_copy(dx, dz, me).start()

    share = BINS // NPER
    mine = jnp.zeros((NODES, share), F32)
    for p in range(NPER):
        mine = jnp.where(per == p, full[:, p * share : (p + 1) * share], mine)
    packed_ref[:NODES, :share] = mine

    for dz in Z_SEND:
        meta_to_z(dz).wait_send()
        outcome_to_z(dz).wait_send()
    for dz in Z_TAKE:
        for dx in X_SEND:
            meta_to_x(dz, dx).wait_send()
            outcome_to_x(dz, dx).wait_send()
    for chunk in range(2):
        for dp in P_SEND:
            part_copy(chunk, dp, per).wait_send()

    for dx, dz in far_first:
        top_copy(dx, dz, row_of(dx, dz)).wait_recv()
    packed_ref[2 * NODES : 2 * NODES + 1, :] = jnp.max(tops[...], axis=0)
    for dx, dz in far_first:
        top_copy(dx, dz, me).wait_send()


def split_results(packed_ref, gains_ref, best_ref, effect_ref):
    gains_ref[...] = packed_ref[:NODES, : BINS // NPER]
    best_ref[...] = packed_ref[2 * NODES : 2 * NODES + 1, :NODES]
    effect_ref[...] = packed_ref[NODES : 2 * NODES, :WEEKS]


def shards(codes, node, chosen, arm, honest, outcome):
    vmem = pl.BlockSpec(memory_space=pltpu.VMEM)
    hbm = pl.BlockSpec(memory_space=pl.ANY)
    dma = pltpu.SemaphoreType.DMA
    packed = pl.pallas_call(
        kernel,
        out_shape=jax.ShapeDtypeStruct((2 * NODES + 8, 128), F32),
        in_specs=[hbm] * 6,
        out_specs=vmem,
        scratch_shapes=[
            pltpu.VMEM((COVARS, UNITS), jnp.int32),
            pltpu.VMEM((1, UNITS), jnp.int32),
            pltpu.VMEM((NODES, SLOTS), jnp.int32),
            pltpu.VMEM((1, UNITS), jnp.int32),
            pltpu.VMEM((1, UNITS), jnp.int32),
            pltpu.VMEM((NROW, WEEKS, UNITS), BF16),
            pltpu.VMEM((NZ, NX, 4, UNITS), BF16),
            pltpu.VMEM((NZ, NX, 4, UNITS), BF16),
            pltpu.VMEM((NROW, 4, UNITS), BF16),
            pltpu.VMEM((2 * HALF + 2 * NODES, BINS), F32),
            pltpu.VMEM((2 * NODES, 2 * WEEKS), F32),
            pltpu.VMEM((2, NPER, 8, BINS), F32),
            pltpu.VMEM((NROW, 1, 128), F32),
            dma((6,)),
            dma((NZ,)),
            dma((NZ,)),
            dma((NROW,)),
            dma((NROW,)),
            dma((NROW,)),
            dma((NZ,)),
            dma((NROW,)),
            dma((2 * NPER,)),
            dma((2 * NPER,)),
            dma((NROW,)),
            dma((NROW,)),
        ],
        compiler_params=pltpu.CompilerParams(collective_id=0, has_side_effects=True),
        name="level",
    )(
        codes.T,
        node.reshape(1, UNITS),
        chosen,
        arm.reshape(1, UNITS),
        honest.reshape(1, UNITS),
        outcome.T,
    )
    gains, best, effect = pl.pallas_call(
        split_results,
        out_shape=(
            jax.ShapeDtypeStruct((NODES, BINS // NPER), F32),
            jax.ShapeDtypeStruct((1, NODES), F32),
            jax.ShapeDtypeStruct((NODES, WEEKS), F32),
        ),
        in_specs=[vmem],
        out_specs=(vmem,) * 3,
        name="split_results",
    )(packed)
    return gains[None], best.reshape(NODES), effect


def solution(mesh):
    in_specs = (P("row", None), P("row"), P(), P("row"), P("row"), P("row", "period"))
    out_specs = (P("row", None, "period"), P(), P(None, "period"))
    return jax.shard_map(shards, mesh=mesh, in_specs=in_specs, out_specs=out_specs, check_vma=False)
```

```python
import jax
import jax.numpy as jnp
from jax import lax
from jax.experimental import pallas as pl
from jax.experimental.pallas import tpu as pltpu
from jax.sharding import PartitionSpec as P

NODES = 16
SLOTS = 32
COVARS = 64
BINS = 256
NX = 4
NZ = 8
NROW = NX * NZ
NPER = 8
UNITS = 256
WEEKS = 16
HALF = NODES * WEEKS
MESH = pl.DeviceIdType.MESH
F32 = jnp.float32
BF16 = jnp.bfloat16
Z_SEND = (4, 3, -3, 2, -2, 1, -1)
Z_TAKE = (0, 1, -1, 2, -2, 3, -3, 4)
X_SEND = (2, 1, 3)
P_SEND = (4, 5, 3, 2, 6, 7, 1)


def kernel(
    codes_hbm,
    node_hbm,
    chosen_hbm,
    arm_hbm,
    honest_hbm,
    outcome_hbm,
    packed_ref,
    codes_ref,
    node_ref,
    chosen_ref,
    arm_ref,
    honest_ref,
    obuf,
    msend,
    mzbuf,
    mxbuf,
    left,
    est,
    parts,
    tops,
    in_sem,
    zo_send,
    zm_send,
    xo_send,
    xm_send,
    o_recv,
    mz_recv,
    mx_recv,
    p_send,
    p_recv,
    t_send,
    t_recv,
):
    me = lax.axis_index("row")
    per = lax.axis_index("period")
    my_x = lax.div(me, NZ)
    my_z = lax.rem(me, NZ)
    z_at = {dz: lax.rem(my_z + (dz + NZ), NZ) for dz in Z_TAKE}
    x_at = {dx: lax.rem(my_x + dx, NX) for dx in range(NX)}

    def row_of(dx, dz):
        return x_at[dx] * NZ + z_at[dz]

    barrier = pltpu.get_barrier_semaphore()
    for dz in Z_SEND:
        pl.semaphore_signal(
            barrier, inc=1, device_id={"row": row_of(0, dz)}, device_id_type=MESH
        )
    for dx in X_SEND:
        pl.semaphore_signal(
            barrier, inc=1, device_id={"row": row_of(dx, 0)}, device_id_type=MESH
        )
    for dp in P_SEND:
        pl.semaphore_signal(
            barrier, inc=1, device_id={"period": lax.rem(per + dp, NPER)}, device_id_type=MESH
        )

    loads = [
        pltpu.make_async_copy(src, dst, in_sem.at[k])
        for k, (src, dst) in enumerate(
            [
                (codes_hbm, codes_ref),
                (node_hbm, node_ref),
                (chosen_hbm, chosen_ref),
                (arm_hbm, arm_ref),
                (honest_hbm, honest_ref),
                (outcome_hbm, obuf.at[me]),
            ]
        )
    ]
    for load in loads:
        load.start()
    for load in loads:
        load.wait()

    node_row = node_ref[...].astype(F32)
    chosen_t = chosen_ref[...].astype(F32).T
    covar = lax.broadcasted_iota(jnp.int32, (SLOTS, COVARS), 1).astype(F32)
    picks = jnp.concatenate(
        [jnp.where(chosen_t[:, n : n + 1] == covar, 1.0, 0.0) for n in range(NODES)], axis=0
    ).astype(BF16)
    by_node = jnp.dot(picks, codes_ref[...].astype(F32).astype(BF16), preferred_element_type=F32)
    picked = jnp.zeros((SLOTS, UNITS), F32)
    for n in range(NODES):
        picked = jnp.where(node_row == n, by_node[n * SLOTS : (n + 1) * SLOTS], picked)
    meta = jnp.concatenate(
        [node_row, arm_ref[...].astype(F32), honest_ref[...].astype(F32)], axis=0
    )
    for s in range(SLOTS):
        msend[s % NZ, s // NZ] = jnp.concatenate([picked[s : s + 1], meta], axis=0).astype(BF16)

    pl.semaphore_wait(barrier, len(Z_SEND) + len(X_SEND) + len(P_SEND))

    def outcome_to_z(dz):
        return pltpu.make_async_remote_copy(
            src_ref=obuf.at[me],
            dst_ref=obuf.at[me],
            send_sem=zo_send.at[dz % NZ],
            recv_sem=o_recv.at[me],
            device_id={"row": row_of(0, dz)},
            device_id_type=MESH,
        )

    def meta_to_z(dz):
        return pltpu.make_async_remote_copy(
            src_ref=msend.at[z_at[dz]],
            dst_ref=mzbuf.at[my_z],
            send_sem=zm_send.at[dz % NZ],
            recv_sem=mz_recv.at[my_z],
            device_id={"row": row_of(0, dz)},
            device_id_type=MESH,
        )

    def outcome_to_x(dz, dx):
        row = row_of(0, dz)
        return pltpu.make_async_remote_copy(
            src_ref=obuf.at[row],
            dst_ref=obuf.at[row],
            send_sem=xo_send.at[(dz % NZ) * NX + dx],
            recv_sem=o_recv.at[row],
            device_id={"row": row_of(dx, 0)},
            device_id_type=MESH,
        )

    def meta_to_x(dz, dx):
        row = row_of(0, dz)
        source = msend.at[my_z] if dz == 0 else mzbuf.at[z_at[dz]]
        return pltpu.make_async_remote_copy(
            src_ref=source.at[x_at[dx]],
            dst_ref=mxbuf.at[row],
            send_sem=xm_send.at[(dz % NZ) * NX + dx],
            recv_sem=mx_recv.at[row],
            device_id={"row": row_of(dx, 0)},
            device_id_type=MESH,
        )

    def outcome_arrived(row):
        pltpu.make_async_remote_copy(
            src_ref=obuf.at[row],
            dst_ref=obuf.at[row],
            send_sem=zo_send.at[0],
            recv_sem=o_recv.at[row],
            device_id={"row": row},
            device_id_type=MESH,
        ).wait_recv()

    for dz in Z_SEND:
        meta_to_z(dz).start()
        outcome_to_z(dz).start()
    for dx in X_SEND:
        meta_to_x(0, dx).start()
        outcome_to_x(0, dx).start()

    left[...] = jnp.zeros_like(left)
    packed_ref[...] = jnp.zeros_like(packed_ref)
    mxbuf[me] = msend[my_z, my_x]
    for dz in Z_TAKE[1:]:
        row = row_of(0, dz)
        pltpu.make_async_remote_copy(
            src_ref=mzbuf.at[z_at[dz]],
            dst_ref=mzbuf.at[z_at[dz]],
            send_sem=zm_send.at[0],
            recv_sem=mz_recv.at[z_at[dz]],
            device_id={"row": row},
            device_id_type=MESH,
        ).wait_recv()
        for dx in X_SEND:
            meta_to_x(dz, dx).start()
        outcome_arrived(row)
        for dx in X_SEND:
            outcome_to_x(dz, dx).start()
        mxbuf[row] = mzbuf[z_at[dz], my_x]

    def load_rows(rows):
        y = jnp.concatenate([obuf[row] for row in rows], axis=1)
        info = jnp.concatenate([mxbuf[row].astype(F32) for row in rows], axis=1)
        return y, [info[k : k + 1] for k in range(4)]

    def spread(row):
        return jnp.broadcast_to(row, (NODES, row.shape[1])).astype(BF16)

    def add_rows(rows):
        y, (pick, node, arm, honest) = load_rows(rows)
        span = y.shape[1]
        away = jnp.full_like(node, float(NODES))
        in_t = spread(jnp.where((arm * honest) > 0.0, node, away))
        in_c = spread(jnp.where(((1.0 - arm) * honest) > 0.0, node, away))
        pick = spread(pick)
        lane = lax.broadcasted_iota(jnp.int32, (NODES, span), 0).astype(F32).astype(BF16)
        one = jnp.ones((NODES, span), BF16)
        zero = jnp.zeros((NODES, span), BF16)
        mask = jnp.concatenate(
            [
                jnp.where(pick <= lane + jnp.asarray(float(k * NODES), BF16), one, zero)
                for k in range(BINS // NODES)
            ],
            axis=0,
        )
        wide = jnp.concatenate(
            [jnp.where(in_t == jnp.asarray(float(n), BF16), y, zero) for n in range(NODES)]
            + [jnp.where(in_c == jnp.asarray(float(n), BF16), y, zero) for n in range(NODES)]
            + [jnp.where(in_t == lane, one, zero), jnp.where(in_c == lane, one, zero)],
            axis=0,
        )
        left[...] += lax.dot_general(
            wide, mask, (((1,), (1,)), ((), ())), preferred_element_type=F32
        )

    add_rows([row_of(0, dz) for dz in Z_TAKE])

    def take_pair(pair, carry):
        rows = []
        for k in range(2):
            step = pair * 2 + k
            dz = ((step + 1) // 2) * (2 * (step % 2) - 1)
            z = lax.rem(my_z + dz + NZ, NZ)
            for dx in X_SEND:
                row = x_at[dx] * NZ + z
                pltpu.make_async_remote_copy(
                    src_ref=mxbuf.at[row],
                    dst_ref=mxbuf.at[row],
                    send_sem=zm_send.at[0],
                    recv_sem=mx_recv.at[row],
                    device_id={"row": row},
                    device_id_type=MESH,
                ).wait_recv()
                outcome_arrived(row)
                rows.append(row)
        add_rows(rows)
        return carry

    lax.fori_loop(0, NZ // 2, take_pair, 0)

    count_t = left[2 * HALF : 2 * HALF + NODES, :]
    count_c = left[2 * HALF + NODES :, :]
    rest_t = count_t[:, BINS - 1 :] - count_t
    rest_c = count_c[:, BINS - 1 :] - count_c
    w_lt = 1.0 / (count_t + 1.0)
    w_lc = 1.0 / (count_c + 1.0)
    w_rt = 1.0 / (rest_t + 1.0)
    w_rc = 1.0 / (rest_c + 1.0)

    def part_copy(chunk, dp, owner):
        return pltpu.make_async_remote_copy(
            src_ref=parts.at[chunk, owner],
            dst_ref=parts.at[chunk, owner],
            send_sem=p_send.at[chunk * NPER + dp],
            recv_sem=p_recv.at[chunk * NPER + owner],
            device_id={"period": lax.rem(per + dp, NPER)},
            device_id_type=MESH,
        )

    for chunk in range(2):
        sums = []
        for n in range(chunk * 8, chunk * 8 + 8):
            lt = left[n * WEEKS : (n + 1) * WEEKS, :]
            lc = left[HALF + n * WEEKS : HALF + (n + 1) * WEEKS, :]
            rt = lt[:, BINS - 1 :] - lt
            rc = lc[:, BINS - 1 :] - lc
            gap = (lt * w_lt[n : n + 1] - lc * w_lc[n : n + 1]) - (
                rt * w_rt[n : n + 1] - rc * w_rc[n : n + 1]
            )
            sums.append(jnp.sum(gap * gap, axis=0, keepdims=True))
        parts[chunk, per] = jnp.concatenate(sums, axis=0)
        for dp in P_SEND:
            part_copy(chunk, dp, per).start()

    est[...] = jnp.zeros_like(est)

    def add_kept(z, carry):
        y, (_, node, arm, honest) = load_rows([x * NZ + z for x in range(NX)])
        span = y.shape[1]
        away = jnp.full_like(node, float(NODES))
        kept_t = spread(jnp.where((arm * (1.0 - honest)) > 0.0, node, away))
        kept_c = spread(jnp.where(((1.0 - arm) * (1.0 - honest)) > 0.0, node, away))
        lane = lax.broadcasted_iota(jnp.int32, (NODES, span), 0).astype(F32).astype(BF16)
        one = jnp.ones((NODES, span), BF16)
        zero = jnp.zeros((NODES, span), BF16)
        kept = jnp.concatenate(
            [jnp.where(kept_t == lane, one, zero), jnp.where(kept_c == lane, one, zero)], axis=0
        )
        est[...] += lax.dot_general(
            kept,
            jnp.concatenate([y, one], axis=0),
            (((1,), (1,)), ((), ())),
            preferred_element_type=F32,
        )
        return carry

    lax.fori_loop(0, NZ, add_kept, 0)
    packed_ref[NODES : 2 * NODES, :WEEKS] = est[:NODES, :WEEKS] / (est[:NODES, WEEKS : WEEKS + 1] + 1.0) - est[
        NODES:, :WEEKS
    ] / (est[NODES:, WEEKS : WEEKS + 1] + 1.0)
    n_l = count_t + count_c
    n_r = rest_t + rest_c
    balance = n_l * n_r / ((n_l + n_r + 1.0) * (n_l + n_r + 1.0))

    spreads = []
    for chunk in range(2):
        for dp in P_SEND:
            part_copy(chunk, dp, lax.rem(per + dp, NPER)).wait_recv()
        total = parts[chunk, 0]
        for p in range(1, NPER):
            total = total + parts[chunk, p]
        spreads.append(total)
    full = balance * jnp.concatenate(spreads, axis=0)

    peak = jnp.max(full, axis=1, keepdims=True)
    diag = lax.broadcasted_iota(jnp.int32, (NODES, 128), 0) == lax.broadcasted_iota(
        jnp.int32, (NODES, 128), 1
    )
    tops[me] = jnp.sum(jnp.where(diag, peak, 0.0), axis=0, keepdims=True)

    far_first = sorted(
        ((dx, dz) for dx in range(NX) for dz in Z_TAKE if dx or dz),
        key=lambda d: -(min(d[0], NX - d[0]) + abs(d[1])),
    )

    def top_copy(dx, dz, owner):
        return pltpu.make_async_remote_copy(
            src_ref=tops.at[owner],
            dst_ref=tops.at[owner],
            send_sem=t_send.at[dx * NZ + dz % NZ],
            recv_sem=t_recv.at[owner],
            device_id={"row": row_of(dx, dz)},
            device_id_type=MESH,
        )

    for dx, dz in far_first:
        top_copy(dx, dz, me).start()

    share = BINS // NPER
    mine = jnp.zeros((NODES, share), F32)
    for p in range(NPER):
        mine = jnp.where(per == p, full[:, p * share : (p + 1) * share], mine)
    packed_ref[:NODES, :share] = mine

    for dz in Z_SEND:
        meta_to_z(dz).wait_send()
        outcome_to_z(dz).wait_send()
    for dz in Z_TAKE:
        for dx in X_SEND:
            meta_to_x(dz, dx).wait_send()
            outcome_to_x(dz, dx).wait_send()
    for chunk in range(2):
        for dp in P_SEND:
            part_copy(chunk, dp, per).wait_send()

    for dx, dz in far_first:
        top_copy(dx, dz, row_of(dx, dz)).wait_recv()
    packed_ref[2 * NODES : 2 * NODES + 1, :] = jnp.max(tops[...], axis=0)
    for dx, dz in far_first:
        top_copy(dx, dz, me).wait_send()


def split_results(packed_ref, gains_ref, best_ref, effect_ref):
    gains_ref[...] = packed_ref[:NODES, : BINS // NPER]
    best_ref[...] = packed_ref[2 * NODES : 2 * NODES + 1, :NODES]
    effect_ref[...] = packed_ref[NODES : 2 * NODES, :WEEKS]


def shards(codes, node, chosen, arm, honest, outcome):
    vmem = pl.BlockSpec(memory_space=pltpu.VMEM)
    hbm = pl.BlockSpec(memory_space=pl.ANY)
    dma = pltpu.SemaphoreType.DMA
    packed = pl.pallas_call(
        kernel,
        out_shape=pltpu.VMEM((2 * NODES + 8, 128), F32),
        in_specs=[hbm] * 6,
        out_specs=vmem,
        scratch_shapes=[
            pltpu.VMEM((COVARS, UNITS), jnp.int32),
            pltpu.VMEM((1, UNITS), jnp.int32),
            pltpu.VMEM((NODES, SLOTS), jnp.int32),
            pltpu.VMEM((1, UNITS), jnp.int32),
            pltpu.VMEM((1, UNITS), jnp.int32),
            pltpu.VMEM((NROW, WEEKS, UNITS), BF16),
            pltpu.VMEM((NZ, NX, 4, UNITS), BF16),
            pltpu.VMEM((NZ, NX, 4, UNITS), BF16),
            pltpu.VMEM((NROW, 4, UNITS), BF16),
            pltpu.VMEM((2 * HALF + 2 * NODES, BINS), F32),
            pltpu.VMEM((2 * NODES, 2 * WEEKS), F32),
            pltpu.VMEM((2, NPER, 8, BINS), F32),
            pltpu.VMEM((NROW, 1, 128), F32),
            dma((6,)),
            dma((NZ,)),
            dma((NZ,)),
            dma((NROW,)),
            dma((NROW,)),
            dma((NROW,)),
            dma((NZ,)),
            dma((NROW,)),
            dma((2 * NPER,)),
            dma((2 * NPER,)),
            dma((NROW,)),
            dma((NROW,)),
        ],
        compiler_params=pltpu.CompilerParams(collective_id=0, has_side_effects=True),
        name="level",
    )(
        codes.T,
        node.reshape(1, UNITS),
        chosen,
        arm.reshape(1, UNITS),
        honest.reshape(1, UNITS),
        outcome.T,
    )
    gains, best, effect = pl.pallas_call(
        split_results,
        out_shape=(
            jax.ShapeDtypeStruct((NODES, BINS // NPER), F32),
            jax.ShapeDtypeStruct((1, NODES), F32),
            jax.ShapeDtypeStruct((NODES, WEEKS), F32),
        ),
        in_specs=[vmem],
        out_specs=(vmem,) * 3,
        name="split_results",
    )(pltpu.with_memory_space_constraint(packed, pltpu.VMEM))
    return gains[None], best.reshape(NODES), effect


def solution(mesh):
    in_specs = (P("row", None), P("row"), P(), P("row"), P("row"), P("row", "period"))
    out_specs = (P("row", None, "period"), P(), P(None, "period"))
    return jax.shard_map(shards, mesh=mesh, in_specs=in_specs, out_specs=out_specs, check_vma=False)
```

```python
import jax
import jax.numpy as jnp
from jax import lax
from jax.experimental import pallas as pl
from jax.experimental.pallas import tpu as pltpu
from jax.sharding import PartitionSpec as P

NODES = 16
SLOTS = 32
COVARS = 64
BINS = 256
NX = 4
NZ = 8
NROW = NX * NZ
NPER = 8
UNITS = 256
WEEKS = 16
HALF = NODES * WEEKS
MESH = pl.DeviceIdType.MESH
F32 = jnp.float32
BF16 = jnp.bfloat16
Z_SEND = (4, 3, -3, 2, -2, 1, -1)
Z_TAKE = (0, 1, -1, 2, -2, 3, -3, 4)
X_SEND = (2, 1, 3)
P_SEND = (4, 5, 3, 2, 6, 7, 1)


def kernel(
    codes_hbm,
    node_hbm,
    chosen_hbm,
    arm_hbm,
    honest_hbm,
    outcome_hbm,
    packed_ref,
    codes_ref,
    node_ref,
    chosen_ref,
    arm_ref,
    honest_ref,
    obuf,
    msend,
    mzbuf,
    mxbuf,
    left,
    est,
    parts,
    tops,
    in_sem,
    zo_send,
    zm_send,
    xo_send,
    xm_send,
    o_recv,
    mz_recv,
    mx_recv,
    p_send,
    p_recv,
    t_send,
    t_recv,
):
    me = lax.axis_index("row")
    per = lax.axis_index("period")
    my_x = lax.div(me, NZ)
    my_z = lax.rem(me, NZ)
    z_at = {dz: lax.rem(my_z + (dz + NZ), NZ) for dz in Z_TAKE}
    x_at = {dx: lax.rem(my_x + dx, NX) for dx in range(NX)}

    def row_of(dx, dz):
        return x_at[dx] * NZ + z_at[dz]

    loads = [
        pltpu.make_async_copy(src, dst, in_sem.at[k])
        for k, (src, dst) in enumerate(
            [
                (codes_hbm, codes_ref),
                (node_hbm, node_ref),
                (chosen_hbm, chosen_ref),
                (arm_hbm, arm_ref),
                (honest_hbm, honest_ref),
                (outcome_hbm, obuf.at[me]),
            ]
        )
    ]
    for load in loads:
        load.start()
    barrier = pltpu.get_barrier_semaphore()
    for dz in Z_SEND:
        pl.semaphore_signal(
            barrier, inc=1, device_id={"row": row_of(0, dz)}, device_id_type=MESH
        )
    for dx in X_SEND:
        pl.semaphore_signal(
            barrier, inc=1, device_id={"row": row_of(dx, 0)}, device_id_type=MESH
        )
    for dp in P_SEND:
        pl.semaphore_signal(
            barrier, inc=1, device_id={"period": lax.rem(per + dp, NPER)}, device_id_type=MESH
        )

    for load in loads:
        load.wait()

    node_row = node_ref[...].astype(F32)
    chosen_t = chosen_ref[...].astype(F32).T
    covar = lax.broadcasted_iota(jnp.int32, (SLOTS, COVARS), 1).astype(F32)
    picks = jnp.concatenate(
        [jnp.where(chosen_t[:, n : n + 1] == covar, 1.0, 0.0) for n in range(NODES)], axis=0
    ).astype(BF16)
    by_node = jnp.dot(picks, codes_ref[...].astype(F32).astype(BF16), preferred_element_type=F32)
    picked = jnp.zeros((SLOTS, UNITS), F32)
    for n in range(NODES):
        picked = jnp.where(node_row == n, by_node[n * SLOTS : (n + 1) * SLOTS], picked)
    meta = jnp.concatenate(
        [node_row, arm_ref[...].astype(F32), honest_ref[...].astype(F32)], axis=0
    )
    for s in range(SLOTS):
        msend[s % NZ, s // NZ] = jnp.concatenate([picked[s : s + 1], meta], axis=0).astype(BF16)

    pl.semaphore_wait(barrier, len(Z_SEND) + len(X_SEND) + len(P_SEND))

    def outcome_to_z(dz):
        return pltpu.make_async_remote_copy(
            src_ref=obuf.at[me],
            dst_ref=obuf.at[me],
            send_sem=zo_send.at[dz % NZ],
            recv_sem=o_recv.at[me],
            device_id={"row": row_of(0, dz)},
            device_id_type=MESH,
        )

    def meta_to_z(dz):
        return pltpu.make_async_remote_copy(
            src_ref=msend.at[z_at[dz]],
            dst_ref=mzbuf.at[my_z],
            send_sem=zm_send.at[dz % NZ],
            recv_sem=mz_recv.at[my_z],
            device_id={"row": row_of(0, dz)},
            device_id_type=MESH,
        )

    def outcome_to_x(dz, dx):
        row = row_of(0, dz)
        return pltpu.make_async_remote_copy(
            src_ref=obuf.at[row],
            dst_ref=obuf.at[row],
            send_sem=xo_send.at[(dz % NZ) * NX + dx],
            recv_sem=o_recv.at[row],
            device_id={"row": row_of(dx, 0)},
            device_id_type=MESH,
        )

    def meta_to_x(dz, dx):
        row = row_of(0, dz)
        source = msend.at[my_z] if dz == 0 else mzbuf.at[z_at[dz]]
        return pltpu.make_async_remote_copy(
            src_ref=source.at[x_at[dx]],
            dst_ref=mxbuf.at[row],
            send_sem=xm_send.at[(dz % NZ) * NX + dx],
            recv_sem=mx_recv.at[row],
            device_id={"row": row_of(dx, 0)},
            device_id_type=MESH,
        )

    def outcome_arrived(row):
        pltpu.make_async_remote_copy(
            src_ref=obuf.at[row],
            dst_ref=obuf.at[row],
            send_sem=zo_send.at[0],
            recv_sem=o_recv.at[row],
            device_id={"row": row},
            device_id_type=MESH,
        ).wait_recv()

    for dz in Z_SEND:
        meta_to_z(dz).start()
        outcome_to_z(dz).start()
    for dx in X_SEND:
        meta_to_x(0, dx).start()
        outcome_to_x(0, dx).start()

    left[...] = jnp.zeros_like(left)
    packed_ref[...] = jnp.zeros_like(packed_ref)
    mxbuf[me] = msend[my_z, my_x]
    for dz in Z_TAKE[1:]:
        row = row_of(0, dz)
        pltpu.make_async_remote_copy(
            src_ref=mzbuf.at[z_at[dz]],
            dst_ref=mzbuf.at[z_at[dz]],
            send_sem=zm_send.at[0],
            recv_sem=mz_recv.at[z_at[dz]],
            device_id={"row": row},
            device_id_type=MESH,
        ).wait_recv()
        for dx in X_SEND:
            meta_to_x(dz, dx).start()
        outcome_arrived(row)
        for dx in X_SEND:
            outcome_to_x(dz, dx).start()
        mxbuf[row] = mzbuf[z_at[dz], my_x]

    def load_rows(rows):
        y = jnp.concatenate([obuf[row] for row in rows], axis=1)
        info = jnp.concatenate([mxbuf[row].astype(F32) for row in rows], axis=1)
        return y, [info[k : k + 1] for k in range(4)]

    def spread(row):
        return jnp.broadcast_to(row, (NODES, row.shape[1])).astype(BF16)

    def add_rows(rows):
        y, (pick, node, arm, honest) = load_rows(rows)
        span = y.shape[1]
        away = jnp.full_like(node, float(NODES))
        in_t = spread(jnp.where((arm * honest) > 0.0, node, away))
        in_c = spread(jnp.where(((1.0 - arm) * honest) > 0.0, node, away))
        pick = spread(pick)
        lane = lax.broadcasted_iota(jnp.int32, (NODES, span), 0).astype(F32).astype(BF16)
        one = jnp.ones((NODES, span), BF16)
        zero = jnp.zeros((NODES, span), BF16)
        mask = jnp.concatenate(
            [
                jnp.where(pick <= lane + jnp.asarray(float(k * NODES), BF16), one, zero)
                for k in range(BINS // NODES)
            ],
            axis=0,
        )
        wide = jnp.concatenate(
            [jnp.where(in_t == jnp.asarray(float(n), BF16), y, zero) for n in range(NODES)]
            + [jnp.where(in_c == jnp.asarray(float(n), BF16), y, zero) for n in range(NODES)]
            + [jnp.where(in_t == lane, one, zero), jnp.where(in_c == lane, one, zero)],
            axis=0,
        )
        left[...] += lax.dot_general(
            wide, mask, (((1,), (1,)), ((), ())), preferred_element_type=F32
        )

    add_rows([row_of(0, dz) for dz in Z_TAKE])

    def take_pair(pair, carry):
        rows = []
        for k in range(2):
            step = pair * 2 + k
            dz = ((step + 1) // 2) * (2 * (step % 2) - 1)
            z = lax.rem(my_z + dz + NZ, NZ)
            for dx in X_SEND:
                row = x_at[dx] * NZ + z
                pltpu.make_async_remote_copy(
                    src_ref=mxbuf.at[row],
                    dst_ref=mxbuf.at[row],
                    send_sem=zm_send.at[0],
                    recv_sem=mx_recv.at[row],
                    device_id={"row": row},
                    device_id_type=MESH,
                ).wait_recv()
                outcome_arrived(row)
                rows.append(row)
        add_rows(rows)
        return carry

    lax.fori_loop(0, NZ // 2, take_pair, 0)

    count_t = left[2 * HALF : 2 * HALF + NODES, :]
    count_c = left[2 * HALF + NODES :, :]
    rest_t = count_t[:, BINS - 1 :] - count_t
    rest_c = count_c[:, BINS - 1 :] - count_c
    w_lt = 1.0 / (count_t + 1.0)
    w_lc = 1.0 / (count_c + 1.0)
    w_rt = 1.0 / (rest_t + 1.0)
    w_rc = 1.0 / (rest_c + 1.0)

    def part_copy(chunk, dp, owner):
        return pltpu.make_async_remote_copy(
            src_ref=parts.at[chunk, owner],
            dst_ref=parts.at[chunk, owner],
            send_sem=p_send.at[chunk * NPER + dp],
            recv_sem=p_recv.at[chunk * NPER + owner],
            device_id={"period": lax.rem(per + dp, NPER)},
            device_id_type=MESH,
        )

    for chunk in range(2):
        sums = []
        for n in range(chunk * 8, chunk * 8 + 8):
            lt = left[n * WEEKS : (n + 1) * WEEKS, :]
            lc = left[HALF + n * WEEKS : HALF + (n + 1) * WEEKS, :]
            rt = lt[:, BINS - 1 :] - lt
            rc = lc[:, BINS - 1 :] - lc
            gap = (lt * w_lt[n : n + 1] - lc * w_lc[n : n + 1]) - (
                rt * w_rt[n : n + 1] - rc * w_rc[n : n + 1]
            )
            sums.append(jnp.sum(gap * gap, axis=0, keepdims=True))
        parts[chunk, per] = jnp.concatenate(sums, axis=0)
        for dp in P_SEND:
            part_copy(chunk, dp, per).start()

    est[...] = jnp.zeros_like(est)

    def add_kept(z, carry):
        y, (_, node, arm, honest) = load_rows([x * NZ + z for x in range(NX)])
        span = y.shape[1]
        away = jnp.full_like(node, float(NODES))
        kept_t = spread(jnp.where((arm * (1.0 - honest)) > 0.0, node, away))
        kept_c = spread(jnp.where(((1.0 - arm) * (1.0 - honest)) > 0.0, node, away))
        lane = lax.broadcasted_iota(jnp.int32, (NODES, span), 0).astype(F32).astype(BF16)
        one = jnp.ones((NODES, span), BF16)
        zero = jnp.zeros((NODES, span), BF16)
        kept = jnp.concatenate(
            [jnp.where(kept_t == lane, one, zero), jnp.where(kept_c == lane, one, zero)], axis=0
        )
        est[...] += lax.dot_general(
            kept,
            jnp.concatenate([y, one], axis=0),
            (((1,), (1,)), ((), ())),
            preferred_element_type=F32,
        )
        return carry

    lax.fori_loop(0, NZ, add_kept, 0)
    packed_ref[NODES : 2 * NODES, :WEEKS] = est[:NODES, :WEEKS] / (est[:NODES, WEEKS : WEEKS + 1] + 1.0) - est[
        NODES:, :WEEKS
    ] / (est[NODES:, WEEKS : WEEKS + 1] + 1.0)
    n_l = count_t + count_c
    n_r = rest_t + rest_c
    balance = n_l * n_r / ((n_l + n_r + 1.0) * (n_l + n_r + 1.0))

    spreads = []
    for chunk in range(2):
        for dp in P_SEND:
            part_copy(chunk, dp, lax.rem(per + dp, NPER)).wait_recv()
        total = parts[chunk, 0]
        for p in range(1, NPER):
            total = total + parts[chunk, p]
        spreads.append(total)
    full = balance * jnp.concatenate(spreads, axis=0)

    peak = jnp.max(full, axis=1, keepdims=True)
    diag = lax.broadcasted_iota(jnp.int32, (NODES, 128), 0) == lax.broadcasted_iota(
        jnp.int32, (NODES, 128), 1
    )
    tops[me] = jnp.sum(jnp.where(diag, peak, 0.0), axis=0, keepdims=True)

    far_first = sorted(
        ((dx, dz) for dx in range(NX) for dz in Z_TAKE if dx or dz),
        key=lambda d: -(min(d[0], NX - d[0]) + abs(d[1])),
    )

    def top_copy(dx, dz, owner):
        return pltpu.make_async_remote_copy(
            src_ref=tops.at[owner],
            dst_ref=tops.at[owner],
            send_sem=t_send.at[dx * NZ + dz % NZ],
            recv_sem=t_recv.at[owner],
            device_id={"row": row_of(dx, dz)},
            device_id_type=MESH,
        )

    for dx, dz in far_first:
        top_copy(dx, dz, me).start()

    share = BINS // NPER
    mine = jnp.zeros((NODES, share), F32)
    for p in range(NPER):
        mine = jnp.where(per == p, full[:, p * share : (p + 1) * share], mine)
    packed_ref[:NODES, :share] = mine

    for dz in Z_SEND:
        meta_to_z(dz).wait_send()
        outcome_to_z(dz).wait_send()
    for dz in Z_TAKE:
        for dx in X_SEND:
            meta_to_x(dz, dx).wait_send()
            outcome_to_x(dz, dx).wait_send()
    for chunk in range(2):
        for dp in P_SEND:
            part_copy(chunk, dp, per).wait_send()

    for dx, dz in far_first:
        top_copy(dx, dz, row_of(dx, dz)).wait_recv()
    packed_ref[2 * NODES : 2 * NODES + 1, :] = jnp.max(tops[...], axis=0)
    for dx, dz in far_first:
        top_copy(dx, dz, me).wait_send()


def split_results(packed_ref, gains_ref, best_ref, effect_ref):
    gains_ref[...] = packed_ref[:NODES, : BINS // NPER]
    best_ref[...] = packed_ref[2 * NODES : 2 * NODES + 1, :NODES]
    effect_ref[...] = packed_ref[NODES : 2 * NODES, :WEEKS]


def shards(codes, node, chosen, arm, honest, outcome):
    vmem = pl.BlockSpec(memory_space=pltpu.VMEM)
    hbm = pl.BlockSpec(memory_space=pl.ANY)
    dma = pltpu.SemaphoreType.DMA
    packed = pl.pallas_call(
        kernel,
        out_shape=pltpu.VMEM((2 * NODES + 8, 128), F32),
        in_specs=[hbm] * 6,
        out_specs=vmem,
        scratch_shapes=[
            pltpu.VMEM((COVARS, UNITS), jnp.int32),
            pltpu.VMEM((1, UNITS), jnp.int32),
            pltpu.VMEM((NODES, SLOTS), jnp.int32),
            pltpu.VMEM((1, UNITS), jnp.int32),
            pltpu.VMEM((1, UNITS), jnp.int32),
            pltpu.VMEM((NROW, WEEKS, UNITS), BF16),
            pltpu.VMEM((NZ, NX, 4, UNITS), BF16),
            pltpu.VMEM((NZ, NX, 4, UNITS), BF16),
            pltpu.VMEM((NROW, 4, UNITS), BF16),
            pltpu.VMEM((2 * HALF + 2 * NODES, BINS), F32),
            pltpu.VMEM((2 * NODES, 2 * WEEKS), F32),
            pltpu.VMEM((2, NPER, 8, BINS), F32),
            pltpu.VMEM((NROW, 1, 128), F32),
            dma((6,)),
            dma((NZ,)),
            dma((NZ,)),
            dma((NROW,)),
            dma((NROW,)),
            dma((NROW,)),
            dma((NZ,)),
            dma((NROW,)),
            dma((2 * NPER,)),
            dma((2 * NPER,)),
            dma((NROW,)),
            dma((NROW,)),
        ],
        compiler_params=pltpu.CompilerParams(collective_id=0, has_side_effects=True),
        name="level",
    )(
        codes.T,
        node.reshape(1, UNITS),
        chosen,
        arm.reshape(1, UNITS),
        honest.reshape(1, UNITS),
        outcome.T,
    )
    gains, best, effect = pl.pallas_call(
        split_results,
        out_shape=(
            jax.ShapeDtypeStruct((NODES, BINS // NPER), F32),
            jax.ShapeDtypeStruct((1, NODES), F32),
            jax.ShapeDtypeStruct((NODES, WEEKS), F32),
        ),
        in_specs=[vmem],
        out_specs=(vmem,) * 3,
        name="split_results",
    )(pltpu.with_memory_space_constraint(packed, pltpu.VMEM))
    return gains[None], best.reshape(NODES), effect


def solution(mesh):
    in_specs = (P("row", None), P("row"), P(), P("row"), P("row"), P("row", "period"))
    out_specs = (P("row", None, "period"), P(), P(None, "period"))
    return jax.shard_map(shards, mesh=mesh, in_specs=in_specs, out_specs=out_specs, check_vma=False)
```
